32 devices in a mesh: clip: 2 (over x), tile: 16 (over z, y, core).
Axes of the slice: x: 2, y: 2, z: 4, core: 2. Of those that a mesh axis runs over, the one named last changes fastest.
Arguments:
- latent: bfloat16 [8, 128, 32, 128], P('clip', 'tile'), parts along dimension 0, may hold values from -6 to 6
- cotangent: bfloat16 [8, 256, 64, 128], P('clip', 'tile'), parts along dimension 0, may hold values from -6 to 6
- kernel: bfloat16 [3, 3, 3, 128, 128], replicated, may hold values from -0.109375 to 0.109375
- ramp_lengths: int32 [32], P('clip'), parts along dimension 0, may hold values from 1 to 4
Outputs:
- latent_grad: bfloat16 [8, 128, 32, 128], P('clip', 'tile'), parts along dimension 0
- kernel_grad: float32 [256, 3456], P(('clip', 'tile')), parts along dimension 0
The draws below stay inside these ranges and needn't reach their ends.
There are 2 independent parts, one for each index of `clip`. The reference program is written for one: setup_inputs(seed, part) draws one part's arguments, and reference() takes and returns one part's arrays. A program takes and returns all parts, laid end to end along the dimension named above; an argument that names none is the same for every part. Nothing has to cross between parts.
Inputs may be any that keep to these rules, and one draw needn't show every extreme that they name: `ramp_lengths`: entry t (t >= 1) is the ramp length of the boundary between tiles t - 1 and t; entry 0 is not used.
All inputs are finite; a program needn't handle non-finite values.
Results may differ from the reference program's by a relative error of at most 0.0031.
Values may be sent and summed in bfloat16 or wider, within the bound.
A program may use at most 128 MiB of HBM per device.

```python
import math
import jax
import jax.numpy as jnp
from jax import lax

C = 128
F = 4
R = 8
COLS = 32
OV = 1
NR = 128
N_TILE = 16


def place_ends(values, key, smallest, top_value):
    index_at = [jax.random.randint(jax.random.fold_in(key, axis), (), 0, length) for axis, length in enumerate(values.shape)]
    main_axis = values.shape.index(max(values.shape))
    beside = index_at[:main_axis] + [(index_at[main_axis] + 1) % values.shape[main_axis]] + index_at[main_axis + 1:]
    return values.at[tuple(index_at)].set(smallest).at[tuple(beside)].set(top_value)


def levels(key, extent, cuts, least, high):
    factor_of, own = 1.0, jax.random.fold_in(key, 6)
    for position, parts in cuts:
        heights = jnp.exp(jax.random.uniform(jax.random.fold_in(own, position), (parts,), jnp.float32, least / len(cuts), high / len(cuts)))
        factor_of = factor_of * jnp.repeat(heights, extent[position] // parts).reshape([-1 if axis == position else 1 for axis in range(len(extent))])
    return factor_of


def normal_values(own_key, shape, deviation, most, pieces=(), kind=jnp.bfloat16):
    values = deviation * jax.random.normal(own_key, shape, jnp.float32)
    if pieces:
        values = values * levels(own_key, shape, pieces, -0.22, 0.18)
    return jnp.clip(values, -most, most).astype(kind)


def setup_inputs(seed: int = 0, part: int = 0) -> dict:
    splits = jax.random.split(jax.random.key(seed), 5)
    own_keys = jax.random.split(jax.random.fold_in(splits[4], part), 5)
    return {
        "latent": normal_values(own_keys[0], (F, NR, COLS, C), 1.0, 6.0, ((1, 16),)),
        "cotangent": normal_values(own_keys[1], (F, 2 * NR, 2 * COLS, C), 1.0, 6.0, ((1, 16),)),
        "kernel": normal_values(splits[2], (3, 3, 3, C, C), (27 * C) ** -0.5, 0.109375),
        "ramp_lengths": place_ends(jax.random.randint(own_keys[3], (N_TILE,), 1, 4 * OV + 1), jax.random.fold_in(own_keys[3], 1), 1, 4 * OV).astype(jnp.int32),
    }


def rise(offset, length):
    shift_rows = (4 * OV - length) // 2
    value = (offset - shift_rows + 1).astype(jnp.float32) / (length + 1).astype(jnp.float32)
    return jnp.clip(value, 0.0, 1.0)

def blend_rows(rows_local, band_out, tile_id, tiles, ramp_lengths):
    lower_len = ramp_lengths[tile_id]
    upper_len = ramp_lengths[jnp.minimum(tile_id + 1, tiles - 1)]
    low_factor = jnp.where(tile_id >= 1, rise(rows_local, lower_len), jnp.float32(1.0))
    high_factor = jnp.where(tile_id <= tiles - 2, 1.0 - rise(rows_local - band_out, upper_len), jnp.float32(1.0))
    return (low_factor * high_factor).astype(jnp.float32)

def upsample(values):
    return jnp.repeat(jnp.repeat(values, 2, axis=1), 2, axis=2)

def spread_back(grad_rows, kernel):
    frames, rows_n, width, chans = grad_rows.shape
    padded = jnp.pad(grad_rows, ((0, 2), (2, 2), (1, 1), (0, 0)))
    summed = jnp.zeros((frames * (rows_n + 2) * width, chans), jnp.float32)
    for frame_tap in range(3):
        for row_tap in range(3):
            for col_tap in range(3):
                window = padded[2 - frame_tap:2 - frame_tap + frames, 2 - row_tap:2 - row_tap + rows_n + 2, 2 - col_tap:2 - col_tap + width]
                summed = summed + lax.dot_general(window.reshape(-1, chans), kernel[frame_tap, row_tap, col_tap], (((1,), (1,)), ((), ())), preferred_element_type=jnp.float32)
    return summed.reshape(frames, rows_n + 2, width, chans)

def kernel_terms(grad_rows, up_rows, chan_first, chan_count):
    frames, rows_n, width, chans = grad_rows.shape
    padded = jnp.pad(up_rows, ((2, 0), (0, 0), (1, 1), (0, 0)))
    padded = lax.dynamic_slice_in_dim(padded, chan_first, chan_count, 3)
    flat_grad = grad_rows.reshape(-1, chans)
    blocks = []
    for frame_tap in range(3):
        for row_tap in range(3):
            for col_tap in range(3):
                window = padded[frame_tap:frame_tap + frames, row_tap:row_tap + rows_n, col_tap:col_tap + width]
                blocks.append(lax.dot_general(window.reshape(-1, chan_count), flat_grad, (((0,), (0,)), ((), ())), preferred_element_type=jnp.float32))
    return jnp.concatenate(blocks, axis=1)

def pool_pairs(values):
    frames, rows_n, width, chans = values.shape
    return values.reshape(frames, rows_n // 2, 2, width // 2, 2, chans).sum(axis=(2, 4))

def reference(latent, cotangent, kernel, ramp_lengths):
    frames, rows_all, width, chans = latent.shape
    tiles = N_TILE
    ext_rows = 2 * R + 4 * OV
    lat_pad = jnp.pad(latent, ((0, 0), (OV, OV), (0, 0), (0, 0)))
    cot_pad = jnp.pad(cotangent, ((0, 0), (2 * OV, 2 * OV), (0, 0), (0, 0)))
    rows_local = jnp.arange(ext_rows, dtype=jnp.int32)

    def one_tile(carry, tile_id):
        grad_sum, kernel_sum = carry
        lat_ext = lax.dynamic_slice_in_dim(lat_pad, (tile_id * R).astype(jnp.int32), R + 2 * OV, 1)
        cot_ext = lax.dynamic_slice_in_dim(cot_pad, (tile_id * 2 * R).astype(jnp.int32), ext_rows, 1)
        weights = blend_rows(rows_local, 2 * R, tile_id, tiles, ramp_lengths)
        grad_w = (cot_ext.astype(jnp.float32) * weights[None, :, None, None]).astype(jnp.bfloat16)
        up_pad = jnp.pad(upsample(lat_ext), ((0, 0), (1, 1), (0, 0), (0, 0)))
        grad_up = spread_back(grad_w, kernel)[:, 1:ext_rows + 1]
        pooled = pool_pairs(grad_up)
        offset = (tile_id * R).astype(jnp.int32)
        current = lax.dynamic_slice_in_dim(grad_sum, offset, R + 2 * OV, 1)
        grad_sum = lax.dynamic_update_slice_in_dim(grad_sum, current + pooled, offset, 1)
        kernel_sum = kernel_sum + kernel_terms(grad_w, up_pad, 0, chans)
        return ((grad_sum, kernel_sum), None)
    init = (jnp.zeros((frames, rows_all + 2 * OV, width, chans), jnp.float32), jnp.zeros((chans, 27 * chans), jnp.float32))
    (grad_sum, kernel_sum), unused = lax.scan(one_tile, init, jnp.arange(tiles, dtype=jnp.int32))
    latent_grad = grad_sum[:, OV:OV + rows_all].astype(jnp.bfloat16)
    kernel_grad = kernel_sum / jnp.float32(math.sqrt(4 * frames * rows_all * width))
    return (latent_grad, kernel_grad)
```

```python
import functools
import math

import jax
import jax.numpy as jnp
from jax import lax
from jax.experimental import pallas as pl
from jax.experimental.pallas import tpu as pltpu
from jax.sharding import PartitionSpec as P

OV = 1
MESH = pl.DeviceIdType.MESH
F32 = jnp.float32
BF16 = jnp.bfloat16


def rise(offset, length):
    shift_rows = lax.shift_right_arithmetic(4 * OV - length, jnp.ones_like(length))
    value = (offset - shift_rows + 1).astype(F32) / (length + 1).astype(F32)
    return jnp.clip(value, 0.0, 1.0)


def pooling(width):
    wide = 2 * width
    out = []
    for group in range(2):
        c = lax.broadcasted_iota(jnp.int32, (width, 4 * wide), 0)
        w = lax.broadcasted_iota(jnp.int32, (width, 4 * wide), 1) - 2 * group * wide
        inside = (w >= 0) & (w < 2 * wide)
        w = jnp.where(w >= wide, w - wide, w)
        for kc in range(3):
            gap = w - 2 * c
            hit = inside & ((gap == 1 - kc) | (gap == 2 - kc))
            out.append(jnp.where(hit, 1.0, 0.0).astype(BF16))
    return jnp.concatenate(out, axis=0)


def body(tiles, fused, norm, ramp_in, lat_in, cot_in, k_in, lg_ref, kg_ref, *scratch):
    (ramp_ref, lat_ref, cot_ref, k_ref, in_sem, cot_sem, halo_lo, halo_hi, lat_halo, s_ref, lhs, edge_lhs,
     g_ref, edge_ref, kt_ref, halo_send, halo_recv) = scratch[:17]
    if fused:
        (part, core_buf, y_send, y_recv, z_send, z_recv, core_ss, core_rs, y_ss, y_rs, z_ss, z_rs) = scratch[17:]
    frames, band, width, chans = lat_ref.shape
    wide = 2 * width
    area = band * width
    span = 3 * chans
    me = lax.axis_index("tile")
    core = lax.rem(me, 2)
    chip = lax.div(me, 2)
    y = lax.rem(chip, 2)
    z = lax.div(chip, 2)
    mine = 1 - core
    layers = tiles // 4
    half = layers // 2

    copies = [pltpu.make_async_copy(cot_in.at[f], cot_ref.at[f], cot_sem.at[f]) for f in range(frames)]
    ramp_copy = pltpu.make_async_copy(ramp_in, ramp_ref, in_sem.at[0])
    lat_copy = pltpu.make_async_copy(lat_in, lat_ref, in_sem.at[1])
    k_copy = pltpu.make_async_copy(k_in, k_ref, in_sem.at[2])
    for f in range(frames):
        copies[f].start()
    lat_copy.start()
    ramp_copy.start()
    k_copy.start()

    barrier = pltpu.get_barrier_semaphore()

    def greet(tile):
        pl.semaphore_signal(barrier, inc=1, device_id={"tile": tile}, device_id_type=MESH)

    if fused:
        for d in range(1, 2 * layers):
            other = lax.rem(2 * z + core + d, 2 * layers)
            greet(4 * lax.div(other, 2) + 2 * y + lax.rem(other, 2))
        greet(4 * z + 2 * (1 - y) + core)
        beyond = me - 1 + 2 * core
        has_beyond = (beyond >= 0) & (beyond < tiles)

        @pl.when(has_beyond)
        def _():
            greet(beyond)

        greeted = 2 * layers + jnp.where(has_beyond, 1, 0)
    else:
        @pl.when(me > 0)
        def _():
            greet(me - 1)

        @pl.when(me < tiles - 1)
        def _():
            greet(me + 1)

        greeted = jnp.where(me > 0, 1, 0) + jnp.where(me < tiles - 1, 1, 0)

    @pl.when(me == 0)
    def _():
        halo_lo[...] = jnp.zeros_like(halo_lo)

    @pl.when(me == tiles - 1)
    def _():
        halo_hi[...] = jnp.zeros_like(halo_hi)
        lat_halo[...] = jnp.zeros_like(lat_halo)

    def halo(src, dst, k, tile):
        return pltpu.make_async_remote_copy(
            src_ref=src, dst_ref=dst, send_sem=halo_send.at[k], recv_sem=halo_recv.at[k],
            device_id={"tile": tile}, device_id_type=MESH,
        )

    below, above = lax.rem(me + tiles - 1, tiles), lax.rem(me + 1, tiles)
    cot_down = halo(cot_in.at[:, 0], halo_hi, 0, below)
    lat_down = halo(lat_in.at[:, 0], lat_halo, 1, below)
    cot_up = halo(cot_in.at[:, 2 * band - 1], halo_lo, 2, above)

    def meet():
        pl.semaphore_wait(barrier, greeted)

        @pl.when(me > 0)
        def _():
            cot_down.start()
            lat_down.start()

        @pl.when(me < tiles - 1)
        def _():
            cot_up.start()

    last_chip = chip == tiles // 2 - 1

    @pl.when(last_chip)
    def _():
        meet()

    s_ref[...] = pooling(width)

    def put(block, kr, f, q):
        for kc in range(3):
            rows = slice(f * area + q * width, f * area + (q + 1) * width)
            g_ref[rows, kr * span + kc * chans : kr * span + (kc + 1) * chans] = block[kc]

    def boxes(pair, rows_of, targets):
        right = jnp.concatenate([rows_of(f) for f in pair], axis=1)
        groups = right.shape[0] // (2 * wide)
        left = s_ref[: 3 * width * groups, : 2 * wide * groups]
        res = jnp.dot(left, right, preferred_element_type=F32).astype(BF16)
        for n, f in enumerate(pair):
            for group in range(groups):
                base = 3 * width * group
                block = [
                    res[base + kc * width : base + (kc + 1) * width, n * chans : (n + 1) * chans] for kc in range(3)
                ]
                for kr, q in targets[group]:
                    if kr is None:
                        for kc in range(3):
                            edge_ref[f * width : (f + 1) * width, kc * chans : (kc + 1) * chans] = block[kc]
                    else:
                        put(block, kr, f, q)

    def whole_rows(first, count):
        return lambda f: cot_ref[f, first : first + count].reshape(count * wide, chans)

    pairs = [(f, f + 1) for f in range(0, frames, 2)]

    for pair in pairs:
        for f in pair:
            copies[f].wait()
        for q in range(0, band, 2):
            boxes(pair, whole_rows(2 * q, 4), ([(1, q)], [(1, q + 1)]))
    lat_copy.wait()
    for f in range(frames):
        turned = lat_ref[f].reshape(area, chans).T
        for kt in range(3):
            g_frame = f + 2 - kt
            if g_frame < frames:
                lhs[kt * chans : (kt + 1) * chans, g_frame * area : (g_frame + 1) * area] = turned
    for kt in range(2):
        for g_frame in range(2 - kt):
            lhs[kt * chans : (kt + 1) * chans, g_frame * area : (g_frame + 1) * area] = jnp.zeros(
                (chans, area), BF16
            )

    share = 8 if not fused else part.shape[3]

    def store_part(kr, total, add):
        for kt in range(3):
            if fused:
                for owner in range(tiles):
                    start = kt * chans + owner * share
                    value = total[start : start + share]
                    if add:
                        value = value + part[kr, owner, kt]
                    part[kr, owner, kt] = value
            else:
                cols = slice((kt * 3 + kr) * span, (kt * 3 + kr + 1) * span)
                value = total[kt * chans : (kt + 1) * chans]
                if add:
                    value = value + kg_ref[:, cols]
                kg_ref[:, cols] = value

    def kernel_part(kr):
        store_part(
            kr, jnp.dot(lhs[...], g_ref[:, kr * span : (kr + 1) * span], preferred_element_type=F32), False
        )

    def core_copy(kr, n):
        theirs = pl.ds(core * 4 * half + 4 * n, 4)
        return pltpu.make_async_remote_copy(
            src_ref=part.at[kr, theirs], dst_ref=core_buf.at[kr, n], send_sem=core_ss.at[kr, n],
            recv_sem=core_rs.at[kr, n], device_id={"tile": 2 * chip + 1 - core}, device_id_type=MESH,
        )

    def y_copy(kr, n):
        return pltpu.make_async_remote_copy(
            src_ref=y_send.at[kr, n], dst_ref=y_recv.at[kr, n], send_sem=y_ss.at[kr, n],
            recv_sem=y_rs.at[kr, n], device_id={"tile": 4 * z + 2 * (1 - y) + core}, device_id_type=MESH,
        )

    def z_copy(kr, n, k):
        target = 4 * (mine * half + n) + 2 * y + k
        return target, pltpu.make_async_remote_copy(
            src_ref=z_send.at[kr, n, k], dst_ref=z_recv.at[kr, z], send_sem=z_ss.at[kr, n, k],
            recv_sem=z_rs.at[kr, z], device_id={"tile": target}, device_id_type=MESH,
        )

    def to_core(kr):
        if fused:
            for n in range(half):
                core_copy(kr, n).start()

    def to_y(kr, n):
        core_copy(kr, n).wait_recv()
        for k in range(2):
            own = part[kr, mine * 4 * half + 4 * n + 2 * (1 - y) + k]
            y_send[kr, n, k] = (own + core_buf[kr, n, 2 * (1 - y) + k]).astype(BF16)
        y_copy(kr, n).start()

    def to_z(kr, n):
        y_copy(kr, n).wait_recv()
        for k in range(2):
            own = part[kr, mine * 4 * half + 4 * n + 2 * y + k]
            z_send[kr, n, k] = (own + core_buf[kr, n, 2 * y + k] + y_recv[kr, n, k].astype(F32)).astype(BF16)
        for k in range(2):
            target, copy = z_copy(kr, n, k)

            @pl.when(target != me)
            def _():
                copy.start()

            @pl.when(target == me)
            def _():
                z_recv[kr, z] = z_send[kr, n, k]

    kernel_part(1)

    @pl.when(jnp.logical_not(last_chip))
    def _():
        meet()

    to_core(1)

    ramp_copy.wait()
    upper = jnp.full((1, chans), ramp_ref[lax.min(me + 1, tiles - 1)], jnp.int32)
    lower = jnp.full((1, chans), ramp_ref[me], jnp.int32)
    has_upper = jnp.where(me <= tiles - 2, 1.0, 0.0).astype(F32)
    has_lower = jnp.where(me >= 1, 1.0, 0.0).astype(F32)
    upper_w = 1.0 - has_upper * rise(jnp.zeros_like(upper), upper)
    lower_w = 1.0 - has_lower * (1.0 - rise(jnp.full_like(lower, 3), lower))
    first_w = jnp.where(me == 0, 1.0, 0.0).astype(F32)

    def scaled(f, r, weight):
        return (cot_ref[f, r].astype(F32) * weight).astype(BF16)

    def high_rows(f):
        low = cot_ref[f, 2 * band - 3]
        return jnp.concatenate([low, cot_ref[f, 2 * band - 2], low, scaled(f, 2 * band - 2, upper_w)], axis=0)

    def low_rows(f):
        return jnp.concatenate(
            [scaled(f, 1, lower_w), cot_ref[f, 2], jnp.zeros((wide, chans), BF16), scaled(f, 0, first_w)], axis=0
        )

    for pair in pairs:
        for j in range(1, band - 1, 2):
            first = [(0, j - 1)] if j == 1 else [(2, j), (0, j - 1)]
            boxes(pair, whole_rows(2 * j - 1, 4), (first, [(2, j + 1), (0, j)]))
        boxes(pair, high_rows, ([(2, band - 1)], [(0, band - 2)]))
        boxes(pair, low_rows, ([(2, 1)], [(2, 0)]))
        for f in pair:
            put([jnp.zeros((width, chans), BF16)] * 3, 0, f, band - 1)
    kernel_part(0)
    kernel_part(2)

    if fused:
        for n in range(half):
            to_y(1, n)

    @pl.when(me < tiles - 1)
    def _():
        cot_down.wait_recv()
        lat_down.wait_recv()

    def edge_rows(f):
        return jnp.concatenate([cot_ref[f, 2 * band - 1], halo_hi[f]], axis=0)

    for pair in pairs:
        boxes(pair, edge_rows, ([(0, band - 1), (None, 0)],))
    for n, edge in enumerate((lat_ref[:, band - 1], lat_halo[...])):
        edge = edge.reshape(frames * width, chans)
        for kt in range(3):
            shift = (2 - kt) * width
            moved = edge
            if shift:
                moved = jnp.concatenate([jnp.zeros((shift, chans), BF16), edge[: frames * width - shift]], axis=0)
            edge_lhs[(3 * n + kt) * chans : (3 * n + kt + 1) * chans] = moved.T
    for n, kr in enumerate((0, 2)):
        store_part(
            kr, jnp.dot(edge_lhs[n * span : (n + 1) * span], edge_ref[...], preferred_element_type=F32), True
        )
        to_core(kr)

    k_copy.wait()
    for kr in range(3):
        for kc in range(3):
            for kt in range(3):
                rows = slice((3 * kr + kc) * chans, (3 * kr + kc + 1) * chans)
                kt_ref[rows, kt * chans : (kt + 1) * chans] = k_ref[kt, kr, kc].T

    if fused:
        for n in range(half):
            for kr in (0, 2):
                to_y(kr, n)

    @pl.when(me > 0)
    def _():
        cot_up.wait_recv()

    def first_rows(f):
        return jnp.concatenate([halo_lo[f], cot_ref[f, 0]], axis=0)

    for pair in pairs:
        boxes(pair, first_rows, ([(2, 0)],))

    sums = [None] * frames
    for f in range(frames):
        first_kt = max(0, 2 - f)
        spread = jnp.dot(
            g_ref[f * area : (f + 1) * area], kt_ref[:, first_kt * chans :], preferred_element_type=F32
        )
        for kt in range(first_kt, 3):
            term = spread[:, (kt - first_kt) * chans : (kt - first_kt + 1) * chans]
            target = f - 2 + kt
            sums[target] = term if sums[target] is None else sums[target] + term
        if fused and f == frames // 2 - 1:
            for n in range(half):
                to_z(1, n)
    for f in range(frames):
        lg_ref[f] = sums[f].astype(BF16).reshape(band, width, chans)
    if fused:
        for n in range(half):
            for kr in (0, 2):
                to_z(kr, n)

    @pl.when(me > 0)
    def _():
        cot_down.wait_send()
        lat_down.wait_send()

    @pl.when(me < tiles - 1)
    def _():
        cot_up.wait_send()

    if fused:
        for kr in (1, 0, 2):
            for n in range(half):
                core_copy(kr, n).wait_send()
                y_copy(kr, n).wait_send()
        for kr in (1, 0, 2):
            for s in range(layers):
                handler = jnp.where(z < half, 1, 0)

                @pl.when(jnp.logical_not((z == s) & (core == handler)))
                def _():
                    pltpu.make_async_remote_copy(
                        src_ref=z_send.at[kr, 0, 0], dst_ref=z_recv.at[kr, s], send_sem=z_ss.at[kr, 0, 0],
                        recv_sem=z_rs.at[kr, s], device_id={"tile": above}, device_id_type=MESH,
                    ).wait_recv()
            for kt in range(3):
                total = z_recv[kr, 0, kt].astype(F32)
                for s in range(1, layers):
                    total = total + z_recv[kr, s, kt].astype(F32)
                start = (kt * 3 + kr) * span
                kg_ref[:, start : start + span] = total / F32(norm)
        for kr in range(3):
            for n in range(half):
                for k in range(2):
                    target, copy = z_copy(kr, n, k)

                    @pl.when(target != me)
                    def _():
                        copy.wait_send()


def write_out(lg_in, kg_in, lg_out, kg_out, sem):
    first = pltpu.make_async_copy(lg_in, lg_out, sem.at[0])
    second = pltpu.make_async_copy(kg_in, kg_out, sem.at[1])
    first.start()
    second.start()
    first.wait()
    second.wait()


def shards(tiles, latent, cotangent, kernel, ramp_lengths):
    frames, band, width, chans = latent.shape
    share = chans // tiles
    norm = math.sqrt(4 * frames * band * tiles * width)
    fused = share % 8 == 0 and tiles % 8 == 0
    layers = tiles // 4
    half = layers // 2
    cols = 27 * chans
    span = 3 * chans
    dma = pltpu.SemaphoreType.DMA
    scratch = [
        pltpu.SMEM(ramp_lengths.shape, ramp_lengths.dtype),
        pltpu.VMEM(latent.shape, BF16),
        pltpu.VMEM(cotangent.shape, BF16),
        pltpu.VMEM(kernel.shape, BF16),
        dma((3,)),
        dma((frames,)),
        pltpu.VMEM((frames, 2 * width, chans), BF16),
        pltpu.VMEM((frames, 2 * width, chans), BF16),
        pltpu.VMEM((frames, width, chans), BF16),
        pltpu.VMEM((6 * width, 8 * width), BF16),
        pltpu.VMEM((span, frames * band * width), BF16),
        pltpu.VMEM((2 * span, frames * width), BF16),
        pltpu.VMEM((frames * band * width, 3 * span), BF16),
        pltpu.VMEM((frames * width, span), BF16),
        pltpu.VMEM((3 * span, span), BF16),
        dma((3,)),
        dma((3,)),
    ]
    if fused:
        scratch += [
            pltpu.VMEM((3, tiles, 3, share, span), F32),
            pltpu.VMEM((3, half, 4, 3, share, span), F32),
            pltpu.VMEM((3, half, 2, 3, share, span), BF16),
            pltpu.VMEM((3, half, 2, 3, share, span), BF16),
            pltpu.VMEM((3, half, 2, 3, share, span), BF16),
            pltpu.VMEM((3, layers, 3, share, span), BF16),
            dma((3, half)),
            dma((3, half)),
            dma((3, half)),
            dma((3, half)),
            dma((3, half, 2)),
            dma((3, layers)),
        ]
    vmem = pl.BlockSpec(memory_space=pltpu.VMEM)
    hbm = pl.BlockSpec(memory_space=pltpu.HBM)
    kg_shape = (share if fused else chans, cols)
    results = (jax.ShapeDtypeStruct(latent.shape, BF16), jax.ShapeDtypeStruct(kg_shape, F32))
    latent_grad, kernel_grad = pl.pallas_call(
        functools.partial(body, tiles, fused, norm),
        out_shape=(pltpu.VMEM(latent.shape, BF16), pltpu.VMEM(kg_shape, F32)) if fused else results,
        in_specs=[hbm] * 4,
        out_specs=(vmem, vmem),
        scratch_shapes=scratch,
        compiler_params=pltpu.CompilerParams(
            collective_id=0, has_side_effects=True, vmem_limit_bytes=40 * 2**20
        ),
    )(*(pltpu.with_memory_space_constraint(a, pltpu.HBM) for a in (ramp_lengths, latent, cotangent, kernel)))
    if not fused:
        kernel_grad = lax.psum_scatter(kernel_grad, "tile", scatter_dimension=0, tiled=True) / F32(norm)
        return latent_grad, kernel_grad
    return pl.pallas_call(
        write_out,
        out_shape=results,
        in_specs=[vmem, vmem],
        out_specs=(hbm, hbm),
        scratch_shapes=[dma((2,))],
        compiler_params=pltpu.CompilerParams(vmem_limit_bytes=4 * 2**20),
    )(latent_grad, kernel_grad)


def solution(mesh):
    in_specs = (P("clip", "tile", None, None), P("clip", "tile", None, None), P(), P("clip"))
    out_specs = (P("clip", "tile", None, None), P(("clip", "tile"), None))
    return jax.shard_map(
        functools.partial(shards, mesh.shape["tile"]),
        mesh=mesh, in_specs=in_specs, out_specs=out_specs, check_vma=False,
    )
```
